32 devices in a mesh: grp: 2 (over core), dp: 16 (over z, y, x).
Axes of the slice: x: 2, y: 2, z: 4, core: 2. Of those that a mesh axis runs over, the one named last changes fastest.
Arguments:
- inputs: bfloat16 [8192, 8192], P(('grp', 'dp')), may hold values from -6 to 6
- query_rows: bfloat16 [8192, 4096], P(('grp', 'dp')), may hold values from -8 to 8
- key_rows: bfloat16 [8192, 512], P(('grp', 'dp')), may hold values from -8 to 8
- cotangent: bfloat16 [8192, 4096], P(('grp', 'dp')), may hold values from -6 to 6
- value_weight: bfloat16 [8192, 512], P('dp'), may hold values from -0.0625 to 0.0625
- domain: int32 [8192], P(('grp', 'dp')), may hold values from 0 to 7
- domain_weight: float32 [8], replicated, may hold values from 0.25 to 4
- route_list: int32 [8192], P(('grp', 'dp')), may hold values from 0 to 15, as said below
- document: int32 [8192], P(('grp', 'dp')), may hold values from 0 to 63, as said below
Outputs:
- attended: bfloat16 [8192, 4096], P(('grp', 'dp'))
- query_grad: bfloat16 [8192, 4096], P(('grp', 'dp'))
- key_grad: bfloat16 [8192, 512], P(('grp', 'dp'))
- weight_grad: float32 [8192, 512], P('dp')
The draws below stay inside these ranges and needn't reach their ends.
Inputs may be any that keep to these rules, and one draw needn't show every extreme that they name: `route_list`: within a group, the rows of one device name any one destination at most 24 times; in every group some destination is named exactly 24 times by every device of the group. Rows of one group with the same document number have the same route_list entry.
All inputs are finite; a program needn't handle non-finite values.
Results may differ from the reference program's by a relative error of at most 0.012.
The reference program's roundings to bfloat16 on the way (of `values`, `scaled`, `probs_low`, `grad_scores` and `value_grad`) count: a program that leaves them out, or rounds other values in their place, can miss the bound.
Values may be sent and summed in bfloat16 or wider, within the bound.
No kernel may reach another device: no remote copies, remote signals or barrier semaphores. Data moves between devices by JAX's collectives and lax.ppermute only.
A program may use at most 192 MiB of HBM per device.

```python
import math
import jax
import jax.numpy as jnp
from jax import lax

D = 8192
HEAD_DIM = 128
HEADS = 32
KV_HEADS = 4
TOK_DEV = 256
DOCS = 4
NDOM = 8
SHARDS = 16
CAP = 24
SLOTS = 384
TOKENS = 8192


def plan_rows(key):
    group_count = TOKENS // (TOK_DEV * SHARDS)
    base = jax.random.fold_in(key, 101)
    full_keys = jax.random.split(jax.random.fold_in(base, 1), group_count)
    full_dest = jax.vmap(lambda one_key: jax.random.randint(one_key, (), 0, SHARDS))(full_keys)
    slot_dest = jnp.arange(SHARDS * CAP, dtype=jnp.int32) // CAP

    def one_source(source_key, full):
        first_key, second_key = jax.random.split(source_key)
        score = jax.random.permutation(first_key, SHARDS * CAP).astype(jnp.int32)
        score = jnp.where(slot_dest == full, score - SHARDS * CAP, score)
        chosen = jnp.argsort(score, stable=True)[:TOK_DEV]
        shuffle = jax.random.permutation(second_key, TOK_DEV)
        return slot_dest[chosen][shuffle]
    source_keys = jax.random.split(jax.random.fold_in(base, 2), group_count * SHARDS)
    fulls = jnp.repeat(full_dest, SHARDS)
    routes = jax.vmap(one_source)(source_keys, fulls).astype(jnp.int32)
    extra = jax.random.randint(jax.random.fold_in(base, 3), (group_count * SHARDS, TOK_DEV), 0, DOCS).astype(jnp.int32)
    return (routes.reshape(-1), (routes * DOCS + extra).reshape(-1))


def draw_route_list(key, part):
    return plan_rows(key)[0]


def draw_document(key, part):
    return plan_rows(key)[1]


def draw_query_rows(key, part):
    noise = jax.random.normal(jax.random.fold_in(key, 11), (TOKENS, HEADS * HEAD_DIM), jnp.float32)
    result = noise
    return jnp.clip(result, -8.0, 8.0).astype(jnp.bfloat16)


def draw_key_rows(key, part):
    noise = jax.random.normal(jax.random.fold_in(key, 21), (TOKENS, KV_HEADS * HEAD_DIM), jnp.float32)
    result = noise
    return jnp.clip(result, -8.0, 8.0).astype(jnp.bfloat16)


def plant(entries, stream_key, smallest, largest):
    index_at = [jax.random.randint(jax.random.fold_in(stream_key, axis), (), 0, length) for axis, length in enumerate(entries.shape)]
    main_axis = entries.shape.index(max(entries.shape))
    next_to = index_at[:main_axis] + [(index_at[main_axis] + 1) % entries.shape[main_axis]] + index_at[main_axis + 1:]
    return entries.at[tuple(index_at)].set(smallest).at[tuple(next_to)].set(largest)


def levels(stream_key, dims, cuts, low, largest):
    def one(position, blocks):
        draws = jax.random.uniform(jax.random.fold_in(jax.random.fold_in(stream_key, 6), position), (blocks,), jnp.float32, low / len(cuts), largest / len(cuts))
        return jnp.repeat(jnp.exp(draws), dims[position] // blocks).reshape((-1,) + (1,) * (len(dims) - position - 1))

    factor_of = one(*cuts[0])
    for cut in cuts[1:]:
        factor_of = factor_of * one(*cut)
    return factor_of


def bell_draw(rng, dims, scale, reach, pieces=(), kind=jnp.bfloat16):
    factor_of = levels(rng, dims, pieces, -0.22, 0.18) if pieces else 1.0
    drawn = jax.random.normal(rng, dims, jnp.float32) * scale * factor_of
    return jnp.minimum(jnp.maximum(drawn, -reach), reach).astype(kind)


def setup_inputs(seed: int = 0) -> dict:
    key_list = jax.random.split(jax.random.key(seed), 10)
    inputs = bell_draw(key_list[0], (TOKENS, D), 1.0, 6.0, ((0, 32),))
    query_rows = draw_query_rows(jax.random.fold_in(key_list[9], 71), 0)
    key_rows = draw_key_rows(jax.random.fold_in(key_list[9], 71), 0)
    cotangent = bell_draw(key_list[3], (TOKENS, HEADS * HEAD_DIM), 1.0, 6.0, ((0, 32),))
    value_weight = bell_draw(key_list[4], (D, KV_HEADS * HEAD_DIM), D ** -0.5, 0.0625, ((0, 16),))
    domain = plant(jax.random.randint(key_list[5], (TOKENS,), 0, NDOM), jax.random.fold_in(key_list[5], 1), 0, NDOM - 1).astype(jnp.int32)
    domain_weight = jnp.clip(jnp.exp(jax.random.uniform(key_list[6], (NDOM,), jnp.float32, math.log(0.25), math.log(4.0))), 0.25, 4.0)
    route_list = draw_route_list(jax.random.fold_in(key_list[9], 71), 0)
    document = draw_document(jax.random.fold_in(key_list[9], 71), 0)
    return {"inputs": inputs, "query_rows": query_rows, "key_rows": key_rows, "cotangent": cotangent, "value_weight": value_weight, "domain": domain, "domain_weight": domain_weight, "route_list": route_list, "document": document}


def attend_block(query_block, kv_block, grad_block, doc_block, order_block):
    group_size = HEADS // KV_HEADS
    kv_width = KV_HEADS * HEAD_DIM
    query_f = query_block.astype(jnp.float32).reshape(SLOTS, KV_HEADS, group_size, HEAD_DIM)
    key_f = kv_block[:, :kv_width].astype(jnp.float32).reshape(SLOTS, KV_HEADS, HEAD_DIM)
    value_f = kv_block[:, kv_width:].astype(jnp.float32).reshape(SLOTS, KV_HEADS, HEAD_DIM)
    grad_f = grad_block.astype(jnp.float32).reshape(SLOTS, KV_HEADS, group_size, HEAD_DIM)
    visible = (doc_block[:, None] == doc_block[None, :]) & (order_block[None, :] <= order_block[:, None])
    score_scale = 1.0 / math.sqrt(HEAD_DIM)
    scores = jnp.einsum('ikgc,jkc->kgij', query_f, key_f) * score_scale
    scores = jnp.where(visible[None, None], scores, -jnp.inf)
    row_peak = lax.optimization_barrier(jnp.max(scores, axis=-1, keepdims=True))
    weights = jnp.exp(scores - row_peak)
    probs = weights / lax.optimization_barrier(jnp.sum(weights, axis=-1, keepdims=True))
    probs_low = lax.optimization_barrier(probs.astype(jnp.bfloat16)).astype(jnp.float32)
    attended = jnp.einsum('kgij,jkc->ikgc', probs_low, value_f).astype(jnp.bfloat16)
    prob_grad = jnp.einsum('ikgc,jkc->kgij', grad_f, value_f)
    row_delta = lax.optimization_barrier(jnp.sum(probs * prob_grad, axis=-1, keepdims=True))
    grad_scores = (probs * (prob_grad - row_delta) * score_scale).astype(jnp.bfloat16)
    grad_scores = lax.optimization_barrier(grad_scores).astype(jnp.float32)
    query_back = jnp.einsum('kgij,jkc->ikgc', grad_scores, key_f).astype(jnp.bfloat16)
    key_back = jnp.einsum('kgij,ikgc->jkc', grad_scores, query_f).astype(jnp.bfloat16)
    value_back = jnp.einsum('kgij,ikgc->jkc', probs_low, grad_f).astype(jnp.bfloat16)
    kv_back = jnp.concatenate([key_back.reshape(SLOTS, kv_width), value_back.reshape(SLOTS, kv_width)], axis=1)
    return (attended.reshape(SLOTS, HEADS * HEAD_DIM), query_back.reshape(SLOTS, HEADS * HEAD_DIM), kv_back)

def reference(inputs, query_rows, key_rows, cotangent, value_weight, domain, domain_weight, route_list, document):
    kv_width = KV_HEADS * HEAD_DIM
    q_width = HEADS * HEAD_DIM
    values = jnp.dot(inputs, value_weight, preferred_element_type=jnp.float32).astype(jnp.bfloat16)
    row_scale = domain_weight[domain]
    scaled = (cotangent.astype(jnp.float32) * row_scale[:, None]).astype(jnp.bfloat16)
    group_rows = TOK_DEV * SHARDS
    group_count = TOKENS // group_rows
    row_index = jnp.arange(TOKENS, dtype=jnp.int32)
    order = (row_index % group_rows).astype(jnp.int32)
    source = (row_index // TOK_DEV).astype(jnp.int32)
    group_of = (row_index // group_rows).astype(jnp.int32)
    targets = (route_list.reshape(TOKENS // TOK_DEV, TOK_DEV, 1) == jnp.arange(SHARDS, dtype=jnp.int32)[None, None, :]).astype(jnp.int32)
    running = jnp.cumsum(targets, axis=1).astype(jnp.int32)
    slot_rank = (lax.optimization_barrier(jnp.sum(running * targets, axis=2)).reshape(-1) - 1).astype(jnp.int32)
    slot = (source % SHARDS * CAP + slot_rank).astype(jnp.int32)
    target_row = (group_of * SHARDS + route_list).astype(jnp.int32)
    table = jnp.full((group_count * SHARDS, SLOTS), TOKENS, jnp.int32).at[target_row, slot].set(row_index)
    stacked_kv = jnp.concatenate([key_rows, values], axis=1)

    def one_target(ids):
        valid = ids < TOKENS
        safe = jnp.where(valid, ids, 0).astype(jnp.int32)
        doc_block = jnp.where(valid, document[safe], -1).astype(jnp.int32)
        order_block = jnp.where(valid, order[safe], -1).astype(jnp.int32)
        return attend_block(query_rows[safe], stacked_kv[safe], scaled[safe], doc_block, order_block)
    att_all, query_all, kv_all = lax.map(one_target, table)
    flat_ids = table.reshape(-1)
    attended = jnp.zeros((TOKENS, q_width), jnp.bfloat16).at[flat_ids].set(att_all.reshape(-1, q_width), mode='drop')
    query_grad = jnp.zeros((TOKENS, q_width), jnp.bfloat16).at[flat_ids].set(query_all.reshape(-1, q_width), mode='drop')
    kv_grad = jnp.zeros((TOKENS, 2 * kv_width), jnp.bfloat16).at[flat_ids].set(kv_all.reshape(-1, 2 * kv_width), mode='drop')
    key_grad = kv_grad[:, :kv_width]
    value_grad = kv_grad[:, kv_width:]
    weight_grad = jnp.dot(inputs.T, value_grad, preferred_element_type=jnp.float32) * (1.0 / math.sqrt(TOKENS))
    return (attended, query_grad, key_grad, weight_grad)
```

```python
import functools
import math

import jax
import jax.numpy as jnp
from jax import lax
from jax.experimental import pallas as pl
from jax.experimental.pallas import tpu as pltpu
from jax.sharding import PartitionSpec as P

HEAD_DIM = 128
META_ROWS = 16
MASKED = -1e30
NT = (((1,), (1,)), ((), ()))
TN = (((0,), (0,)), ((), ()))


def score_kernel(kv, group, slot, pos_ref, qdoc_ref, qord_ref, kdoc_ref, kord_ref, k_ref, *rest):
    qg_refs, (p_ref, q_out, g_out, dv_ref, spread) = rest[:kv], rest[kv:]
    route = pl.program_id(0)
    slots = spread.shape[1]
    rows, width = qg_refs[0].shape
    half = width // 2

    @pl.when(route == 0)
    def _():
        for s in range(kv):
            hot = lax.broadcasted_iota(jnp.int32, (slots, rows), 0) == pos_ref[s]
            hot = jnp.where(hot, 1.0, 0.0).astype(jnp.bfloat16)
            for c in range(0, width, 512):
                spread[s, :, c : c + 512] = jnp.dot(
                    hot, qg_refs[s][:, c : c + 512], preferred_element_type=jnp.float32
                )

    base = pl.multiple_of(route * slot, 8)

    def gather_rows(offset):
        pieces = []
        for h in range(group):
            lane = offset + h * HEAD_DIM
            for s in range(kv):
                pieces.append(spread[s, pl.ds(base, slot), lane : lane + HEAD_DIM])
        return jnp.concatenate(pieces, axis=0).astype(jnp.bfloat16)

    query, grad = gather_rows(0), gather_rows(half)
    q_out[0] = query
    g_out[0] = grad
    sources = k_ref.shape[0]
    keys = k_ref[...].reshape(sources * slot, HEAD_DIM).astype(jnp.bfloat16)
    raw = lax.dot_general(keys, query, NT, preferred_element_type=jnp.float32)
    seen = (kdoc_ref[0] == qdoc_ref[0]) & (kord_ref[...] <= qord_ref[...])
    raw = jnp.where(seen, raw, MASKED)
    peak = jnp.max(raw, axis=0, keepdims=True)
    weights = jnp.exp((raw - peak) * (1.0 / math.sqrt(HEAD_DIM)))
    probs = weights * (1.0 / jnp.sum(weights, axis=0, keepdims=True))
    p_ref[0] = probs
    value_back = jnp.dot(probs.astype(jnp.bfloat16), grad, preferred_element_type=jnp.float32)
    dv_ref[...] = value_back.reshape(sources, slot, HEAD_DIM)


def grad_kernel(
    kv, group, slot, pos_ref, p_ref, q_ref, g_ref, k_ref, v_ref, out_ref, dk_ref, att_s, dq_s
):
    route = pl.program_id(0)
    sources = k_ref.shape[0]
    slots, half = att_s.shape[1:]
    rows = out_ref.shape[1]
    keys = k_ref[...].reshape(sources * slot, HEAD_DIM).astype(jnp.bfloat16)
    vals = v_ref[...].reshape(sources * slot, HEAD_DIM).astype(jnp.bfloat16)
    probs = p_ref[0]
    att = lax.dot_general(
        probs.astype(jnp.bfloat16), vals, TN, preferred_element_type=jnp.float32
    )
    prob_grad = lax.dot_general(vals, g_ref[0], NT, preferred_element_type=jnp.float32)
    delta = jnp.sum(probs * prob_grad, axis=0, keepdims=True)
    grad_scores = probs * (prob_grad - delta) * (1.0 / math.sqrt(HEAD_DIM))
    grad_scores = grad_scores.astype(jnp.bfloat16)
    query_back = lax.dot_general(grad_scores, keys, TN, preferred_element_type=jnp.float32)
    key_back = jnp.dot(grad_scores, q_ref[0], preferred_element_type=jnp.float32)
    dk_ref[...] = key_back.reshape(sources, slot, HEAD_DIM)
    base = pl.multiple_of(route * slot, 8)
    for h in range(group):
        for s in range(kv):
            at = (h * kv + s) * slot
            lanes = slice(h * HEAD_DIM, (h + 1) * HEAD_DIM)
            att_s[s, pl.ds(base, slot), lanes] = att[at : at + slot]
            dq_s[s, pl.ds(base, slot), lanes] = query_back[at : at + slot]

    @pl.when(route == pl.num_programs(0) - 1)
    def _():
        for s in range(kv):
            hot = lax.broadcasted_iota(jnp.int32, (rows, slots), 1) == pos_ref[s]
            hot = jnp.where(hot, 1.0, 0.0).astype(jnp.bfloat16)
            for part, ref in enumerate((att_s, dq_s)):
                for c in range(0, half, 512):
                    out_ref[s, :, part * half + c : part * half + c + 512] = jnp.dot(
                        hot,
                        ref[s, :, c : c + 512].astype(jnp.bfloat16),
                        preferred_element_type=jnp.float32,
                    ).astype(jnp.bfloat16)


def whole(shape):
    return pl.BlockSpec(shape, lambda r: (0,) * len(shape), pipeline_mode=pl.Buffered(1))


def by_route(shape):
    return pl.BlockSpec((1,) + shape, lambda r: (r,) + (0,) * len(shape))


def spread_rows(hot, rows):
    return jnp.einsum("srj,sjc->src", hot, rows, preferred_element_type=jnp.float32)


def collect_rows(hot, slots):
    return jnp.einsum(
        "srj,src->sjc", hot, slots.astype(jnp.bfloat16), preferred_element_type=jnp.float32
    ).astype(jnp.bfloat16)


def body(
    inputs,
    query_rows,
    key_rows,
    cotangent,
    value_weight,
    domain,
    domain_weight,
    route_list,
    document,
):
    rows = inputs.shape[0]
    shards = lax.axis_size("dp")
    groups = lax.axis_size("grp")
    kv_width = value_weight.shape[1]
    q_width = query_rows.shape[1]
    kv = kv_width // HEAD_DIM
    group = q_width // kv_width
    planes = shards // kv
    capacity = 3 * rows // (2 * shards)
    slot = -(-capacity // 8) * 8
    slots = slot * shards
    head_width = group * HEAD_DIM
    own = lax.axis_index("dp")
    core = lax.axis_index("grp")
    low = own % kv

    def swap(x, m):
        return lax.ppermute(x, "dp", [(i, i ^ m) for i in range(shards)])

    def climb(x, m):
        return lax.ppermute(x, "dp", [(i, i + m * kv) for i in range(shards - m * kv)])

    def descend(x, m):
        return lax.ppermute(x, "dp", [(i + m * kv, i) for i in range(shards - m * kv)])

    def cross(x):
        return lax.ppermute(x, "grp", [(i, (i + 1) % groups) for i in range(groups)])

    def columns(x, index, width):
        return lax.dynamic_slice_in_dim(x, index * width, width, 1)

    part_rows = value_weight.shape[0] // groups
    weight = lax.all_gather(
        lax.dynamic_slice_in_dim(value_weight, core * part_rows, part_rows, 0),
        ("dp", "grp"),
        axis=0,
        tiled=True,
    )

    target_ones = (route_list[:, None] == jnp.arange(shards, dtype=jnp.int32)[None, :]).astype(
        jnp.bfloat16
    )
    row_ids = jnp.arange(rows, dtype=jnp.int32)
    triangle = (row_ids[:, None] >= row_ids[None, :]).astype(jnp.bfloat16)
    running = jnp.dot(triangle, target_ones, preferred_element_type=jnp.float32)
    rank = jnp.sum(running * target_ones.astype(jnp.float32), axis=1) - 1.0
    meta = jnp.stack(
        [route_list.astype(jnp.float32), rank, document.astype(jnp.float32) + 1.0]
    ).astype(jnp.bfloat16)
    meta = meta.reshape(-1, HEAD_DIM)
    meta = jnp.pad(meta, ((0, META_ROWS - meta.shape[0]), (0, 0)))

    def key_piece(m):
        return jnp.concatenate([columns(key_rows, low ^ m, HEAD_DIM), meta], axis=0)

    plane_keys = jnp.stack([key_piece(0)] + [swap(key_piece(m), m) for m in range(1, kv)])
    all_keys = jnp.concatenate(
        [plane_keys] + [climb(plane_keys, m) for m in range(1, planes)], axis=0
    )

    domain_hits = domain[:, None] == jnp.arange(domain_weight.shape[0], dtype=jnp.int32)[None, :]
    row_scale = jnp.sum(jnp.where(domain_hits, domain_weight[None, :], 0.0), axis=1)

    def query_piece(m):
        part = columns(cotangent, low ^ m, head_width).astype(jnp.float32) * row_scale[:, None]
        return jnp.concatenate(
            [columns(query_rows, low ^ m, head_width), part.astype(jnp.bfloat16)], axis=1
        )

    plane_qg = [query_piece(0)] + [swap(query_piece(m), m) for m in range(1, kv)]
    inputs_other = cross(inputs)

    sources = planes * kv
    table = all_keys[:, rows:].astype(jnp.int32)
    per = rows // HEAD_DIM
    route_of = table[:, :per].reshape(sources, rows)
    rank_of = table[:, per : 2 * per].reshape(sources, rows)
    doc_of = table[:, 2 * per : 3 * per].reshape(sources, rows)
    position = route_of * slot + rank_of
    hits = position[:, None, :] == jnp.arange(slots, dtype=jnp.int32)[None, :, None]
    hot = hits.astype(jnp.bfloat16)
    slot_doc = jnp.sum(jnp.where(hits, doc_of[:, None, :], 0), axis=2)
    by_key = slot_doc.reshape(sources, shards, slot).transpose(1, 0, 2)
    key_doc = by_key.reshape(shards, sources * slot, 1)
    query_doc = by_key[:, :kv].reshape(shards, 1, kv * slot)
    query_doc = jnp.where(query_doc == 0, -1, query_doc)
    query_doc = jnp.tile(query_doc, (1, 1, group))
    plane_order = (
        (jnp.arange(kv, dtype=jnp.int32) ^ low)[:, None] * slot
        + jnp.arange(slot, dtype=jnp.int32)[None, :]
    ).reshape(-1)
    key_order = jnp.concatenate(
        [plane_order, jnp.full(((sources - kv) * slot,), -1, jnp.int32)]
    )[:, None]
    query_order = jnp.tile(plane_order, group)[None, :]

    key_count, query_count = sources * slot, group * kv * slot
    key_slots = spread_rows(hot, all_keys[:, :rows])
    slot_block = pl.BlockSpec((sources, slot, HEAD_DIM), lambda r: (0, r, 0))
    probs, query_slots, grad_slots, value_back = pl.pallas_call(
        functools.partial(score_kernel, kv, group, slot),
        grid=(shards,),
        out_shape=(
            jax.ShapeDtypeStruct((shards, key_count, query_count), jnp.float32),
            jax.ShapeDtypeStruct((shards, query_count, HEAD_DIM), jnp.bfloat16),
            jax.ShapeDtypeStruct((shards, query_count, HEAD_DIM), jnp.bfloat16),
            jax.ShapeDtypeStruct((sources, slots, HEAD_DIM), jnp.float32),
        ),
        in_specs=[
            whole((kv, 1, rows)),
            by_route((1, query_count)),
            whole((1, query_count)),
            by_route((key_count, 1)),
            whole((key_count, 1)),
            slot_block,
        ]
        + [whole((rows, 2 * head_width))] * kv,
        out_specs=(
            by_route((key_count, query_count)),
            by_route((query_count, HEAD_DIM)),
            by_route((query_count, HEAD_DIM)),
            slot_block,
        ),
        scratch_shapes=[pltpu.VMEM((kv, slots, 2 * head_width), jnp.float32)],
        cost_estimate=pl.CostEstimate(
            flops=4 * shards * key_count * query_count * HEAD_DIM
            + 4 * kv * slots * rows * head_width,
            bytes_accessed=4 * shards * key_count * query_count + 16 * kv * rows * head_width,
            transcendentals=shards * key_count * query_count,
        ),
        name="scores",
    )(
        position[:kv, None, :],
        query_doc,
        query_order,
        key_doc,
        key_order,
        key_slots,
        *plane_qg,
    )

    def bring_home(parts):
        total = parts[:kv].astype(jnp.float32)
        for m in range(1, planes):
            total = total + descend(parts[m * kv : (m + 1) * kv], m).astype(jnp.float32)
        total = total.astype(jnp.bfloat16)
        return in_head_order([total[0]] + [swap(total[m], m) for m in range(1, kv)])

    def in_head_order(pieces):
        stacked = jnp.stack(pieces)
        return jnp.concatenate(
            [lax.dynamic_index_in_dim(stacked, h ^ low, 0, keepdims=False) for h in range(kv)],
            axis=1,
        )

    value_grad = bring_home(collect_rows(hot, value_back))
    share = kv_width // groups
    mine = columns(value_grad, core, share)
    theirs = cross(columns(value_grad, (core + 1) % groups, share))
    chip_part = lax.dot_general(inputs, mine, TN, preferred_element_type=jnp.float32)
    chip_part = chip_part + lax.dot_general(
        inputs_other, theirs, TN, preferred_element_type=jnp.float32
    )
    summed = lax.psum_scatter(
        chip_part.astype(jnp.bfloat16), "dp", scatter_dimension=0, tiled=True
    )
    other = cross(summed)
    both = jnp.stack([summed, other])
    grad_scale = 1.0 / math.sqrt(rows * shards * groups)
    weight_grad = (
        jnp.concatenate(
            [lax.dynamic_index_in_dim(both, h ^ core, 0, keepdims=False) for h in range(groups)],
            axis=1,
        ).astype(jnp.float32)
        * grad_scale
    )

    values = jnp.dot(inputs, weight, preferred_element_type=jnp.float32).astype(jnp.bfloat16)

    def value_piece(m):
        return columns(values, low ^ m, HEAD_DIM)

    plane_values = jnp.stack([value_piece(0)] + [swap(value_piece(m), m) for m in range(1, kv)])
    all_values = jnp.concatenate(
        [plane_values] + [climb(plane_values, m) for m in range(1, planes)], axis=0
    )
    value_slots = spread_rows(hot, all_values)
    plane_out, key_back = pl.pallas_call(
        functools.partial(grad_kernel, kv, group, slot),
        grid=(shards,),
        out_shape=(
            jax.ShapeDtypeStruct((kv, rows, 2 * head_width), jnp.bfloat16),
            jax.ShapeDtypeStruct((sources, slots, HEAD_DIM), jnp.float32),
        ),
        in_specs=[
            whole((kv, rows, 1)),
            by_route((key_count, query_count)),
            by_route((query_count, HEAD_DIM)),
            by_route((query_count, HEAD_DIM)),
            slot_block,
            slot_block,
        ],
        out_specs=(whole((kv, rows, 2 * head_width)), slot_block),
        scratch_shapes=[pltpu.VMEM((kv, slots, head_width), jnp.float32)] * 2,
        cost_estimate=pl.CostEstimate(
            flops=8 * shards * key_count * query_count * HEAD_DIM
            + 4 * kv * slots * rows * head_width,
            bytes_accessed=4 * shards * key_count * query_count + 16 * kv * rows * head_width,
            transcendentals=0,
        ),
        name="grads",
    )(position[:kv, :, None], probs, query_slots, grad_slots, key_slots, value_slots)

    home = [plane_out[0]] + [swap(plane_out[m], m) for m in range(1, kv)]
    attended = in_head_order([piece[:, :head_width] for piece in home])
    query_grad = in_head_order([piece[:, head_width:] for piece in home])
    key_grad = bring_home(collect_rows(hot, key_back))
    return (attended, query_grad, key_grad, weight_grad)


def solution(mesh):
    placed = (
        P(("grp", "dp"), None),
        P(("grp", "dp"), None),
        P(("grp", "dp"), None),
        P(("grp", "dp"), None),
        P("dp", None),
        P(("grp", "dp")),
        P(),
        P(("grp", "dp")),
        P(("grp", "dp")),
    )
    return jax.shard_map(
        body,
        mesh=mesh,
        in_specs=placed,
        out_specs=(
            P(("grp", "dp"), None),
            P(("grp", "dp"), None),
            P(("grp", "dp"), None),
            P("dp", None),
        ),
        check_vma=False,
    )
```

```python
import functools
import math

import jax
import jax.numpy as jnp
from jax import lax
from jax.experimental import pallas as pl
from jax.experimental.pallas import tpu as pltpu
from jax.sharding import PartitionSpec as P


HEAD_DIM = 128
META_ROWS = 16
MASKED = -1e30
NT = (((1,), (1,)), ((), ()))
TN = (((0,), (0,)), ((), ()))


def score_kernel(kv, group, slot, pos_ref, qdoc_ref, qord_ref, kdoc_ref, kord_ref, k_ref, *rest):
    qg_refs, (p_ref, q_out, g_out, dv_ref, spread) = rest[:kv], rest[kv:]
    route = pl.program_id(0)
    slots = spread.shape[1]
    rows, width = qg_refs[0].shape
    half = width // 2

    @pl.when(route == 0)
    def _():
        for s in range(kv):
            hot = lax.broadcasted_iota(jnp.int32, (slots, rows), 0) == pos_ref[s]
            hot = jnp.where(hot, 1.0, 0.0).astype(jnp.bfloat16)
            for c in range(0, width, 512):
                spread[s, :, c : c + 512] = jnp.dot(
                    hot, qg_refs[s][:, c : c + 512], preferred_element_type=jnp.float32
                )

    base = pl.multiple_of(route * slot, 8)

    def gather_rows(offset):
        pieces = []
        for h in range(group):
            lane = offset + h * HEAD_DIM
            for s in range(kv):
                pieces.append(spread[s, pl.ds(base, slot), lane : lane + HEAD_DIM])
        return jnp.concatenate(pieces, axis=0).astype(jnp.bfloat16)

    query, grad = gather_rows(0), gather_rows(half)
    q_out[0] = query
    g_out[0] = grad
    sources = k_ref.shape[0]
    keys = k_ref[...].reshape(sources * slot, HEAD_DIM).astype(jnp.bfloat16)
    raw = lax.dot_general(keys, query, NT, preferred_element_type=jnp.float32)
    seen = (kdoc_ref[0] == qdoc_ref[0]) & (kord_ref[...] <= qord_ref[...])
    raw = jnp.where(seen, raw, MASKED)
    peak = jnp.max(raw, axis=0, keepdims=True)
    weights = jnp.exp((raw - peak) * (1.0 / math.sqrt(HEAD_DIM)))
    probs = weights * (1.0 / jnp.sum(weights, axis=0, keepdims=True))
    p_ref[0] = probs
    value_back = jnp.dot(probs.astype(jnp.bfloat16), grad, preferred_element_type=jnp.float32)
    dv_ref[...] = value_back.reshape(sources, slot, HEAD_DIM)


def grad_kernel(
    kv, group, slot, pos_ref, p_ref, q_ref, g_ref, k_ref, v_ref, out_ref, dk_ref, att_s, dq_s
):
    route = pl.program_id(0)
    sources = k_ref.shape[0]
    slots, half = att_s.shape[1:]
    rows = out_ref.shape[1]
    keys = k_ref[...].reshape(sources * slot, HEAD_DIM).astype(jnp.bfloat16)
    vals = v_ref[...].reshape(sources * slot, HEAD_DIM).astype(jnp.bfloat16)
    probs = p_ref[0]
    att = lax.dot_general(
        probs.astype(jnp.bfloat16), vals, TN, preferred_element_type=jnp.float32
    )
    prob_grad = lax.dot_general(vals, g_ref[0], NT, preferred_element_type=jnp.float32)
    delta = jnp.sum(probs * prob_grad, axis=0, keepdims=True)
    grad_scores = probs * (prob_grad - delta) * (1.0 / math.sqrt(HEAD_DIM))
    grad_scores = grad_scores.astype(jnp.bfloat16)
    query_back = lax.dot_general(grad_scores, keys, TN, preferred_element_type=jnp.float32)
    key_back = jnp.dot(grad_scores, q_ref[0], preferred_element_type=jnp.float32)
    dk_ref[...] = key_back.reshape(sources, slot, HEAD_DIM)
    base = pl.multiple_of(route * slot, 8)
    for h in range(group):
        for s in range(kv):
            at = (h * kv + s) * slot
            lanes = slice(h * HEAD_DIM, (h + 1) * HEAD_DIM)
            att_s[s, pl.ds(base, slot), lanes] = att[at : at + slot]
            dq_s[s, pl.ds(base, slot), lanes] = query_back[at : at + slot]

    @pl.when(route == pl.num_programs(0) - 1)
    def _():
        for s in range(kv):
            hot = lax.broadcasted_iota(jnp.int32, (rows, slots), 1) == pos_ref[s]
            hot = jnp.where(hot, 1.0, 0.0).astype(jnp.bfloat16)
            for part, ref in enumerate((att_s, dq_s)):
                for c in range(0, half, 512):
                    out_ref[s, :, part * half + c : part * half + c + 512] = jnp.dot(
                        hot,
                        ref[s, :, c : c + 512].astype(jnp.bfloat16),
                        preferred_element_type=jnp.float32,
                    ).astype(jnp.bfloat16)


def whole(shape):
    return pl.BlockSpec(shape, lambda r: (0,) * len(shape), pipeline_mode=pl.Buffered(1))


def by_route(shape):
    return pl.BlockSpec((1,) + shape, lambda r: (r,) + (0,) * len(shape))


def spread_rows(hot, rows):
    return jnp.einsum("srj,sjc->src", hot, rows, preferred_element_type=jnp.float32)


def collect_rows(hot, slots):
    return jnp.einsum(
        "srj,src->sjc", hot, slots.astype(jnp.bfloat16), preferred_element_type=jnp.float32
    ).astype(jnp.bfloat16)


def step(
    inputs,
    query_rows,
    key_rows,
    cotangent,
    value_weight,
    domain,
    domain_weight,
    route_list,
    document,
):
    rows = inputs.shape[0]
    shards = lax.axis_size("dp")
    groups = lax.axis_size("grp")
    kv_width = value_weight.shape[1]
    q_width = query_rows.shape[1]
    kv = kv_width // HEAD_DIM
    group = q_width // kv_width
    planes = shards // kv
    capacity = 3 * rows // (2 * shards)
    slot = -(-capacity // 8) * 8
    slots = slot * shards
    head_width = group * HEAD_DIM
    own = lax.axis_index("dp")
    core = lax.axis_index("grp")
    low = own % kv

    def swap(x, m):
        return lax.ppermute(x, "dp", [(i, i ^ m) for i in range(shards)])

    def climb(x, m):
        return lax.ppermute(x, "dp", [(i, i + m * kv) for i in range(shards - m * kv)])

    def descend(x, m):
        return lax.ppermute(x, "dp", [(i + m * kv, i) for i in range(shards - m * kv)])

    def cross(x):
        return lax.ppermute(x, "grp", [(i, (i + 1) % groups) for i in range(groups)])

    def columns(x, index, width):
        return lax.dynamic_slice_in_dim(x, index * width, width, 1)

    part_rows = value_weight.shape[0] // groups
    weight_part = lax.dynamic_slice_in_dim(value_weight, core * part_rows, part_rows, 0)
    weight = lax.all_gather(weight_part, ("dp", "grp"), axis=0, tiled=True)

    target_ones = (route_list[:, None] == jnp.arange(shards, dtype=jnp.int32)[None, :]).astype(
        jnp.bfloat16
    )
    row_ids = jnp.arange(rows, dtype=jnp.int32)
    triangle = (row_ids[:, None] >= row_ids[None, :]).astype(jnp.bfloat16)
    running = jnp.dot(triangle, target_ones, preferred_element_type=jnp.float32)
    rank = jnp.sum(running * target_ones.astype(jnp.float32), axis=1) - 1.0
    meta = jnp.stack(
        [route_list.astype(jnp.float32), rank, document.astype(jnp.float32) + 1.0]
    ).astype(jnp.bfloat16)
    meta = meta.reshape(-1, HEAD_DIM)
    meta = jnp.pad(meta, ((0, META_ROWS - meta.shape[0]), (0, 0)))

    def key_piece(m):
        return jnp.concatenate([columns(key_rows, low ^ m, HEAD_DIM), meta], axis=0)

    plane_keys = jnp.stack([key_piece(0)] + [swap(key_piece(m), m) for m in range(1, kv)])
    all_keys = jnp.concatenate(
        [plane_keys] + [climb(plane_keys, m) for m in range(1, planes)], axis=0
    )

    domain_hits = domain[:, None] == jnp.arange(domain_weight.shape[0], dtype=jnp.int32)[None, :]
    row_scale = jnp.sum(jnp.where(domain_hits, domain_weight[None, :], 0.0), axis=1)

    def query_piece(m):
        part = columns(cotangent, low ^ m, head_width).astype(jnp.float32) * row_scale[:, None]
        return jnp.concatenate(
            [columns(query_rows, low ^ m, head_width), part.astype(jnp.bfloat16)], axis=1
        )

    plane_qg = [query_piece(0)] + [swap(query_piece(m), m) for m in range(1, kv)]
    inputs_other = cross(inputs)

    sources = planes * kv
    table = all_keys[:, rows:].astype(jnp.int32)
    per = rows // HEAD_DIM
    route_of = table[:, :per].reshape(sources, rows)
    rank_of = table[:, per : 2 * per].reshape(sources, rows)
    doc_of = table[:, 2 * per : 3 * per].reshape(sources, rows)
    position = route_of * slot + rank_of
    hits = position[:, None, :] == jnp.arange(slots, dtype=jnp.int32)[None, :, None]
    hot = hits.astype(jnp.bfloat16)
    slot_doc = jnp.sum(jnp.where(hits, doc_of[:, None, :], 0), axis=2)
    by_key = slot_doc.reshape(sources, shards, slot).transpose(1, 0, 2)
    key_doc = by_key.reshape(shards, sources * slot, 1)
    query_doc = by_key[:, :kv].reshape(shards, 1, kv * slot)
    query_doc = jnp.where(query_doc == 0, -1, query_doc)
    query_doc = jnp.tile(query_doc, (1, 1, group))
    plane_order = (
        (jnp.arange(kv, dtype=jnp.int32) ^ low)[:, None] * slot
        + jnp.arange(slot, dtype=jnp.int32)[None, :]
    ).reshape(-1)
    key_order = jnp.concatenate(
        [plane_order, jnp.full(((sources - kv) * slot,), -1, jnp.int32)]
    )[:, None]
    query_order = jnp.tile(plane_order, group)[None, :]

    key_count, query_count = sources * slot, group * kv * slot
    key_slots = spread_rows(hot, all_keys[:, :rows])
    slot_block = pl.BlockSpec((sources, slot, HEAD_DIM), lambda r: (0, r, 0))
    probs, query_slots, grad_slots, value_back = pl.pallas_call(
        functools.partial(score_kernel, kv, group, slot),
        grid=(shards,),
        out_shape=(
            jax.ShapeDtypeStruct((shards, key_count, query_count), jnp.float32),
            jax.ShapeDtypeStruct((shards, query_count, HEAD_DIM), jnp.bfloat16),
            jax.ShapeDtypeStruct((shards, query_count, HEAD_DIM), jnp.bfloat16),
            jax.ShapeDtypeStruct((sources, slots, HEAD_DIM), jnp.float32),
        ),
        in_specs=[
            whole((kv, 1, rows)),
            by_route((1, query_count)),
            whole((1, query_count)),
            by_route((key_count, 1)),
            whole((key_count, 1)),
            slot_block,
        ]
        + [whole((rows, 2 * head_width))] * kv,
        out_specs=(
            by_route((key_count, query_count)),
            by_route((query_count, HEAD_DIM)),
            by_route((query_count, HEAD_DIM)),
            slot_block,
        ),
        scratch_shapes=[pltpu.VMEM((kv, slots, 2 * head_width), jnp.float32)],
        cost_estimate=pl.CostEstimate(
            flops=4 * shards * key_count * query_count * HEAD_DIM
            + 4 * kv * slots * rows * head_width,
            bytes_accessed=4 * shards * key_count * query_count + 16 * kv * rows * head_width,
            transcendentals=shards * key_count * query_count,
        ),
        name="scores",
    )(
        position[:kv, None, :],
        query_doc,
        query_order,
        key_doc,
        key_order,
        key_slots,
        *plane_qg,
    )

    def bring_home(parts):
        total = parts[:kv].astype(jnp.float32)
        for m in range(1, planes):
            total = total + descend(parts[m * kv : (m + 1) * kv], m).astype(jnp.float32)
        total = total.astype(jnp.bfloat16)
        return in_head_order([total[0]] + [swap(total[m], m) for m in range(1, kv)])

    def in_head_order(pieces):
        stacked = jnp.stack(pieces)
        return jnp.concatenate(
            [lax.dynamic_index_in_dim(stacked, h ^ low, 0, keepdims=False) for h in range(kv)],
            axis=1,
        )

    value_grad = bring_home(collect_rows(hot, value_back))
    share = kv_width // groups
    mine = columns(value_grad, core, share)
    theirs = cross(columns(value_grad, (core + 1) % groups, share))
    chip_part = lax.dot_general(inputs, mine, TN, preferred_element_type=jnp.float32)
    chip_part = chip_part + lax.dot_general(
        inputs_other, theirs, TN, preferred_element_type=jnp.float32
    )
    chip_part = chip_part.astype(jnp.bfloat16)
    summed = lax.psum_scatter(chip_part, "dp", scatter_dimension=0, tiled=True)
    other = cross(summed)
    both = jnp.stack([summed, other])
    grad_scale = 1.0 / math.sqrt(rows * shards * groups)
    weight_grad = (
        jnp.concatenate(
            [lax.dynamic_index_in_dim(both, h ^ core, 0, keepdims=False) for h in range(groups)],
            axis=1,
        ).astype(jnp.float32)
        * grad_scale
    )

    values = jnp.dot(inputs, weight, preferred_element_type=jnp.float32).astype(jnp.bfloat16)

    def value_piece(m):
        return columns(values, low ^ m, HEAD_DIM)

    plane_values = jnp.stack([value_piece(0)] + [swap(value_piece(m), m) for m in range(1, kv)])
    all_values = jnp.concatenate(
        [plane_values] + [climb(plane_values, m) for m in range(1, planes)], axis=0
    )
    value_slots = spread_rows(hot, all_values)
    plane_out, key_back = pl.pallas_call(
        functools.partial(grad_kernel, kv, group, slot),
        grid=(shards,),
        out_shape=(
            jax.ShapeDtypeStruct((kv, rows, 2 * head_width), jnp.bfloat16),
            jax.ShapeDtypeStruct((sources, slots, HEAD_DIM), jnp.float32),
        ),
        in_specs=[
            whole((kv, rows, 1)),
            by_route((key_count, query_count)),
            by_route((query_count, HEAD_DIM)),
            by_route((query_count, HEAD_DIM)),
            slot_block,
            slot_block,
        ],
        out_specs=(whole((kv, rows, 2 * head_width)), slot_block),
        scratch_shapes=[pltpu.VMEM((kv, slots, head_width), jnp.float32)] * 2,
        cost_estimate=pl.CostEstimate(
            flops=8 * shards * key_count * query_count * HEAD_DIM
            + 4 * kv * slots * rows * head_width,
            bytes_accessed=4 * shards * key_count * query_count + 16 * kv * rows * head_width,
            transcendentals=0,
        ),
        name="grads",
    )(position[:kv, :, None], probs, query_slots, grad_slots, key_slots, value_slots)

    home = [plane_out[0]] + [swap(plane_out[m], m) for m in range(1, kv)]
    attended = in_head_order([piece[:, :head_width] for piece in home])
    query_grad = in_head_order([piece[:, head_width:] for piece in home])
    key_grad = bring_home(collect_rows(hot, key_back))
    return (attended, query_grad, key_grad, weight_grad)


def solution(mesh):
    placed = (
        P(("grp", "dp"), None),
        P(("grp", "dp"), None),
        P(("grp", "dp"), None),
        P(("grp", "dp"), None),
        P("dp", None),
        P(("grp", "dp")),
        P(),
        P(("grp", "dp")),
        P(("grp", "dp")),
    )
    return jax.shard_map(
        step,
        mesh=mesh,
        in_specs=placed,
        out_specs=(
            P(("grp", "dp"), None),
            P(("grp", "dp"), None),
            P(("grp", "dp"), None),
            P("dp", None),
        ),
        check_vma=False,
    )
```
